32 devices in a mesh: seq: 8 (over z, y), head: 4 (over x, core).
Axes of the slice: x: 2, y: 2, z: 4, core: 2. Of those that a mesh axis runs over, the one named last changes fastest.
Arguments:
- queries: bfloat16 [4096, 1024], P('seq', 'head'), may hold values from -6 to 6
- keys: bfloat16 [4096, 1024], P('seq', 'head'), may hold values from -6 to 6
- values: bfloat16 [4096, 1024], P('seq', 'head'), may hold values from -4 to 4
- masked: int32 [4096], P('seq'), may hold values from 0 to 1
- mask_qkv: bfloat16 [3, 1024], P(None, 'head'), may hold values from -5.09375 to 5.09375
- key_bars: int32 [32, 4], P('seq'), may hold values from -1 to 31, as said below
- w_out: bfloat16 [1024, 1536], P('head'), may hold values from -0.1875 to 0.1875
Outputs:
- attn_out: bfloat16 [4096, 1536], P('seq', 'head')
The draws below stay inside these ranges and needn't reach their ends.
Inputs may be any that keep to these rules, and one draw needn't show every extreme that they name: `key_bars`: entry [b, s] is -1 or a bar on the device s - 2 places along seq for s < 2, s - 1 places for s >= 2. Bar b lists bar a in slot s exactly when a lists b in slot 3 - s. No listed bar is b or next to b. The bars of one device list at most 2 bars of any one other device, and some pair of devices reaches 2.
All inputs are finite; a program needn't handle non-finite values.
Results may differ from the reference program's by a relative error of at most 0.009.
Values may be sent and summed in bfloat16 or wider, within the bound.
A program may use at most 64 MiB of HBM per device.

```python
import math
import jax
import jax.numpy as jnp
from jax import lax

D = 1536
HEADS = 16
HD = 64
BAR = 128
R = 2
BARS_DEV = 4
CAP = 2
NBARS = 32
TOKENS = 4096
N_HEAD = 4


def masked_plan(key):
    return (jax.random.randint(jax.random.fold_in(key, 5), (TOKENS,), 0, 3) == 0).astype(jnp.int32)


def draw_masked(key, part):
    return masked_plan(key)


def base_draw(key, salt):
    local_key = jax.random.fold_in(key, salt)
    return jnp.clip(jax.random.normal(jax.random.fold_in(local_key, 1), (TOKENS, HEADS * HD), jnp.float32), -3.0, 3.0) * 1.7


def draw_queries(key, part):
    result = base_draw(key, 31)
    return result.astype(jnp.bfloat16)


def draw_keys(key, part):
    result = base_draw(key, 32)
    return result.astype(jnp.bfloat16)


def draw_key_bars(key, part):
    devices = NBARS // BARS_DEV
    dev_ids = jnp.arange(devices, dtype=jnp.int32)
    levels = jax.random.randint(jax.random.fold_in(key, 11), (devices,), max(CAP // 2, 1), CAP + 1)
    levels = jnp.where(dev_ids <= R, CAP, levels).astype(jnp.int32)
    table = jnp.full((NBARS, 2 * R), -1, jnp.int32)
    local_ids = jnp.arange(BARS_DEV, dtype=jnp.int32)
    for offset in range(1, R + 1):
        pairs = devices - offset
        counts = jnp.minimum(levels[:pairs], levels[offset:])
        offset_key = jax.random.fold_in(key, 20 + offset)
        send_score = jax.random.randint(jax.random.fold_in(offset_key, 1), (pairs, BARS_DEV), 0, 2 ** 20) * BARS_DEV + local_ids[None, :]
        if offset == 1:
            send_score = jnp.where(local_ids[None, :] == BARS_DEV - 1, 2 ** 30, send_score)
        recv_score = jax.random.randint(jax.random.fold_in(offset_key, 2), (pairs, BARS_DEV), 0, 2 ** 20) * BARS_DEV + local_ids[None, :]
        send_order = jnp.argsort(send_score, axis=1, stable=True).astype(jnp.int32)
        recv_order = jnp.argsort(recv_score, axis=1, stable=True).astype(jnp.int32)
        live = local_ids[None, :] < counts[:, None]
        sender = dev_ids[:pairs, None] * BARS_DEV + send_order
        receiver = (dev_ids[:pairs, None] + offset) * BARS_DEV + recv_order
        table = table.at[sender.reshape(-1), R + offset - 1].set(jnp.where(live, receiver, -1).reshape(-1))
        table = table.at[receiver.reshape(-1), R - offset].set(jnp.where(live, sender, -1).reshape(-1))
    return table


def block_levels(own_key, dims, split, low, top_value):
    loudness = 1.0
    for axis_at, blocks in split:
        steps = jax.random.uniform(jax.random.fold_in(jax.random.fold_in(own_key, 6), axis_at), (blocks,), jnp.float32, low / len(split), top_value / len(split))
        loudness = loudness * jnp.repeat(jnp.exp(steps), dims[axis_at] // blocks).reshape((-1,) + (1,) * (len(dims) - 1 - axis_at))
    return loudness


def gaussian(own_key, shape, spread, most, cuts=(), kind=jnp.bfloat16):
    drawn = spread * jax.random.normal(own_key, shape, jnp.float32)
    if cuts:
        drawn = drawn * block_levels(own_key, shape, cuts, -0.22, 0.18)
    return jnp.clip(drawn, -most, most).astype(kind)


def setup_inputs(seed: int = 0) -> dict:
    splits = jax.random.split(jax.random.key(seed), 8)
    return {
        "queries": draw_queries(jax.random.fold_in(splits[7], 71), 0),
        "keys": draw_keys(jax.random.fold_in(splits[7], 71), 0),
        "values": gaussian(splits[2], (TOKENS, HEADS * HD), 1.0, 4.0, ((0, 8), (1, 4))),
        "masked": draw_masked(jax.random.fold_in(splits[7], 71), 0),
        "mask_qkv": gaussian(splits[4], (3, HEADS * HD), 1.7, 5.09375, ((1, 4),)),
        "key_bars": draw_key_bars(jax.random.fold_in(splits[7], 71), 0),
        "w_out": gaussian(splits[6], (HEADS * HD, D), (HEADS * HD) ** -0.5, 0.1875, ((0, 4),)),
    }


def attend_group(query_grp, key_grp, value_grp, usable):
    scaling = 1.0 / math.sqrt(HD)
    scores = jnp.einsum('gqhd,gnkhd->ghqnk', query_grp.astype(jnp.float32), key_grp.astype(jnp.float32)) * scaling
    scores = jnp.where(usable[:, None, None, :, None], scores, -jnp.inf)
    row_max = lax.optimization_barrier(jnp.max(scores, axis=(3, 4), keepdims=True))
    raised = jnp.exp(scores - row_max)
    totals = lax.optimization_barrier(jnp.sum(raised, axis=(3, 4)))
    rounded = lax.optimization_barrier(raised.astype(jnp.bfloat16)).astype(jnp.float32)
    weighted = jnp.einsum('ghqnk,gnkhd->gqhd', rounded, value_grp.astype(jnp.float32))
    return (weighted / jnp.transpose(totals, (0, 2, 1))[..., None]).astype(jnp.bfloat16)

def reference(queries, keys, values, masked, mask_qkv, key_bars, w_out):
    flagged = (masked == 1)[:, None]
    query_eff = jnp.where(flagged, mask_qkv[0][None, :], queries)
    key_eff = jnp.where(flagged, mask_qkv[1][None, :], keys)
    value_eff = jnp.where(flagged, mask_qkv[2][None, :], values)
    shaped = (NBARS, BAR, HEADS, HD)
    query_blocks = query_eff.reshape(shaped)
    key_blocks = key_eff.reshape(shaped)
    value_blocks = value_eff.reshape(shaped)
    bar_ids = jnp.arange(NBARS, dtype=jnp.int32)
    band_ids = jnp.stack([bar_ids - 1, bar_ids, bar_ids + 1], axis=1)
    listed = jnp.concatenate([band_ids, key_bars.astype(jnp.int32)], axis=1).astype(jnp.int32)
    usable = jnp.concatenate([(band_ids >= 0) & (band_ids < NBARS), key_bars >= 0], axis=1)
    listed = jnp.clip(listed, 0, NBARS - 1)
    group_size = 8

    def one_group(start):
        row_ids = start + jnp.arange(group_size, dtype=jnp.int32)
        picked = listed[row_ids]
        return attend_group(query_blocks[row_ids], key_blocks[picked], value_blocks[picked], usable[row_ids])
    starts = jnp.arange(0, NBARS, group_size, dtype=jnp.int32)
    attended = lax.map(one_group, starts).reshape(TOKENS, HEADS * HD)
    head_split = HEADS * HD // N_HEAD
    summed = jnp.zeros((TOKENS, D), jnp.float32)
    for member in range(N_HEAD):
        partial_value = jnp.dot(attended[:, member * head_split:(member + 1) * head_split], w_out[member * head_split:(member + 1) * head_split], preferred_element_type=jnp.float32)
        summed = summed + lax.optimization_barrier(partial_value.astype(jnp.bfloat16)).astype(jnp.float32)
    return summed.astype(jnp.bfloat16)
```

```python
import functools

import jax
import jax.numpy as jnp
from jax import lax
from jax.experimental import pallas as pl
from jax.experimental.pallas import tpu as pltpu
from jax.sharding import PartitionSpec as P

HD = 64
CAP = 2
LANES = 128
MESH = pl.DeviceIdType.MESH
NEG = -1e30


def kernel(
    n_seq, n_head, bars_hbm, masked_hbm, mask_hbm, q_hbm, k_hbm, v_hbm, w_hbm, out_hbm,
    bars, twin_bars, masked_ref, mask_ref, raw, own, give, twin, near, back, pack_own, pack_twin,
    pick_near, pick_far, q_own, q_give, q_twin, w_all, att, att_twin, part, out_ref, acc, top, tot,
    out_sem, small_sem, load_sem, w_own, bars_send, bars_recv, give_send, give_recv, q_send, q_recv,
    near_send, near_recv, back_send, back_recv, pick_send, pick_recv,
    w_send, w_recv, y_send, y_recv, att_send, att_recv,
):
    seq = lax.axis_index("seq")
    head = lax.axis_index("head")
    n_bar, bar_len, out_cols = out_ref.shape
    odd = lax.rem(seq, 2)
    other = 1 - odd
    partner = seq + 1 - 2 * odd
    outer = seq - 2 + 4 * odd
    inner = seq + 2 - 4 * odd
    has_outer = jnp.logical_and(outer >= 0, outer < n_seq)
    has_inner = jnp.logical_and(inner >= 0, inner < n_seq)
    per_tile = LANES // HD

    def slot_bar(i):
        return i + odd * (n_bar - 1 - 2 * i)

    def column(c, count):
        return c + odd * (count - 1 - 2 * c)

    def column_twin(c, count):
        return column(c, count)

    columns = bars.shape[1]

    barrier = pltpu.get_barrier_semaphore()
    peers = [lax.rem(head + step, n_head) for step in range(1, n_head)]
    count = n_head
    for there, place in ((has_outer, outer), (has_inner, inner)):
        count = count + there.astype(jnp.int32)

        @pl.when(there)
        def _(place=place):
            pl.semaphore_signal(barrier, inc=1, device_id=(place, head), device_id_type=MESH)

    pl.semaphore_signal(barrier, inc=1, device_id=(partner, head), device_id_type=MESH)
    for peer in peers:
        pl.semaphore_signal(barrier, inc=1, device_id=(seq, peer), device_id_type=MESH)

    small = [
        pltpu.make_async_copy(source, target, small_sem.at[n])
        for n, (source, target) in enumerate(
            ((masked_hbm, masked_ref), (mask_hbm, mask_ref), (bars_hbm, bars))
        )
    ]
    for load in small:
        load.start()
    loads = [
        pltpu.make_async_copy(source, raw.at[n], load_sem.at[n])
        for n, source in enumerate((k_hbm, v_hbm, q_hbm))
    ]
    for load in loads:
        load.start()
    own_w = pltpu.make_async_copy(
        w_hbm.at[:, pl.ds(pl.multiple_of(head * out_cols, LANES), out_cols)], w_all.at[head], w_own
    )
    own_w.start()

    rows = lax.broadcasted_iota(jnp.int32, (bar_len, bar_len), 0)
    cols = lax.broadcasted_iota(jnp.int32, (bar_len, bar_len), 1)
    lane = lax.broadcasted_iota(jnp.int32, (bar_len, LANES), 1)
    mine = pl.ds(pl.multiple_of(odd * LANES, LANES), LANES)
    theirs = pl.ds(pl.multiple_of(other * LANES, LANES), LANES)

    for load in small:
        load.wait()
    hits = {}

    def flag(i):
        row = masked_ref[pl.ds(slot_bar(i), 1), :]
        hits[i] = jnp.max(jnp.where(rows == cols, row, 0), axis=1, keepdims=True) == 1

    def replaced(n, i, row, tile):
        mask_row = mask_ref[row : row + 1, tile].astype(jnp.float32)
        return jnp.where(hits[i], mask_row, raw[n, slot_bar(i), :, tile].astype(jnp.float32))

    def prepare(target, i, tile):
        target[i, :, :LANES] = replaced(0, i, 1, tile).astype(jnp.bfloat16)
        target[i, :, LANES:] = replaced(1, i, 2, tile).astype(jnp.bfloat16)

    def send(source, target, send_sem, recv_sem, place):
        return pltpu.make_async_remote_copy(
            src_ref=source, dst_ref=target, send_sem=send_sem, recv_sem=recv_sem,
            device_id=place, device_id_type=MESH,
        )

    def give_copy(i):
        return send(give.at[i], twin.at[i], give_send, give_recv.at[i], (partner, head))

    give_all = send(give, twin, give_send, give_recv.at[0], (partner, head))
    q_all = send(q_give, q_twin, q_send, q_recv, (partner, head))
    near_all = send(own, near, near_send, near_recv, (outer, head))
    back_all = send(twin, back, back_send, back_recv, (inner, head))

    def near_copy(i):
        return send(own.at[i], near.at[i], near_send, near_recv, (outer, head))

    def back_copy(i):
        return send(twin.at[i], back.at[i], back_send, back_recv, (inner, head))

    def pick_copy(far):
        if far:
            return send(pack_twin, pick_far, pick_send.at[1], pick_recv.at[1], (outer, head))
        return send(pack_own, pick_near, pick_send.at[0], pick_recv.at[0], (inner, head))

    bars_copy = pltpu.make_async_remote_copy(
        src_ref=bars_hbm, dst_ref=twin_bars, send_sem=bars_send, recv_sem=bars_recv,
        device_id=(partner, head), device_id_type=MESH,
    )

    core = head + 1 - 2 * lax.rem(head, 2)
    across = lax.rem(head + 2, n_head)
    turn = lax.rem(seq // 2, 2)
    direct = across + turn * (1 - 2 * lax.rem(across, 2))
    mate = seq + 2 - 4 * turn

    def w_copy(step):
        if step == 2:
            source, target, place = w_all.at[direct], w_all.at[direct], (mate, head)
        else:
            peer = direct if step else core
            source = w_hbm.at[:, pl.ds(pl.multiple_of(peer * out_cols, LANES), out_cols)]
            target, place = w_all.at[head], (seq, peer)
        return send(source, target, w_send, w_recv.at[step], place)

    loads[0].wait()
    loads[1].wait()
    for i in range(n_bar):
        flag(i)
        prepare(give, i, theirs)
        prepare(own, i, mine)
        if i == 0:
            pl.semaphore_wait(barrier, count)
            bars_copy.start()
        give_copy(i).start()

        @pl.when(has_outer)
        def _(i=i):
            near_copy(i).start()

    for step in (1, 0):
        w_copy(step).start()

    def picks(table, c, turned):
        before = jnp.int32(0)
        chosen = [jnp.int32(0)] * CAP
        for b in range(n_bar):
            used = (table[b, c] >= 0).astype(jnp.int32)
            at = b + odd * (n_bar - 1 - 2 * b)
            if turned:
                at = n_bar - 1 - at
            for slot in range(CAP):
                chosen[slot] = chosen[slot] + jnp.where(before == slot, used * at, 0)
            before = before + used
        return chosen

    for slot, at in enumerate(picks(bars, column(columns - 1, columns), False)):
        pack_own[slot] = own[at]

    @pl.when(has_inner)
    def _():
        pick_copy(0).start()

    loads[2].wait()
    for i in range(n_bar):
        q_give[i] = (replaced(2, i, 0, theirs) * HD ** -0.5).astype(jnp.bfloat16)
    for i in range(n_bar):
        q_own[i] = (replaced(2, i, 0, mine) * HD ** -0.5).astype(jnp.bfloat16)

    @pl.when(jnp.logical_not(has_outer))
    def _():
        back[...] = jnp.zeros(back.shape, back.dtype)
        pick_near[...] = jnp.zeros(pick_near.shape, pick_near.dtype)

    @pl.when(jnp.logical_not(has_inner))
    def _():
        near[...] = jnp.zeros(near.shape, near.dtype)
        pick_far[...] = jnp.zeros(pick_far.shape, pick_far.dtype)

    for i in range(n_bar):
        give_copy(i).wait_recv()
        if i == 1:
            q_all.start()

        @pl.when(has_inner)
        def _(i=i):
            back_copy(i).start()

    bars_copy.wait_recv()
    for slot, at in enumerate(picks(twin_bars, column(0, columns), True)):
        pack_twin[slot] = twin[at]

    @pl.when(has_outer)
    def _():
        pick_copy(1).start()

    w_copy(1).wait_recv()
    w_copy(2).start()

    halves = [(lane // HD == h).astype(jnp.bfloat16) for h in range(per_tile)]

    def weigh(jobs):
        scores = []
        for query, blocks, _ in jobs:
            stacked = jnp.concatenate([query * half for half in halves], axis=0)
            row = []
            for block, usable in blocks:
                s = lax.dot_general(
                    stacked, block[:, :LANES], (((1,), (1,)), ((), ())), preferred_element_type=jnp.float32
                )
                if usable is not None:
                    s = s + jnp.where(usable, 0.0, NEG).astype(jnp.float32)
                row.append(s)
            scores.append(row)
        peaks, fades = [], []
        for row, (_, _, old) in zip(scores, jobs):
            peak = jnp.max(functools.reduce(jnp.maximum, row), axis=1, keepdims=True)
            if old is not None:
                peak = jnp.maximum(peak, top[old])
                fades.append(jnp.exp(top[old] - peak))
            else:
                fades.append(None)
            peaks.append(peak)
        totals, rounded = [], []
        for row, peak, fade, (_, _, old) in zip(scores, peaks, fades, jobs):
            raised = [jnp.exp(s - peak) for s in row]
            total = jnp.sum(functools.reduce(jnp.add, raised), axis=1, keepdims=True)
            if old is not None:
                total = total + tot[old] * fade
            totals.append(total)
            rounded.append(jnp.concatenate([r.astype(jnp.bfloat16) for r in raised], axis=1))
        sums = []
        for weight, fade, (_, blocks, old) in zip(rounded, fades, jobs):
            value = jnp.concatenate([block[:, LANES:] for block, _ in blocks], axis=0)
            weighted = jnp.dot(weight, value, preferred_element_type=jnp.float32)
            if old is not None:
                weighted = weighted + acc[old] * fade
            sums.append(weighted)
        return list(zip(peaks, totals, sums))

    def keep(slots, states):
        for slot, (peak, total, weighted) in zip(slots, states):
            top[slot] = jnp.broadcast_to(peak, top.shape[1:])
            tot[slot] = jnp.broadcast_to(total, tot.shape[1:])
            acc[slot] = weighted

    def finish(state):
        _, total, weighted = state
        done = weighted / total
        result = done[:bar_len]
        for h in range(1, per_tile):
            result = jnp.where(lane // HD == h, done[h * bar_len : (h + 1) * bar_len], result)
        return result.astype(jnp.bfloat16)

    def whole(table, b, c, ref, turned):
        wanted = table[b, c]
        at = lax.rem(jnp.maximum(wanted, 0), n_bar)
        at = at + odd * (n_bar - 1 - 2 * at)
        if turned:
            at = n_bar - 1 - at
        return ref[at], wanted >= 0

    def picked(table, b, c, ref):
        wanted = table[b, c]
        slot = jnp.int32(0)
        for o in range(n_bar):
            held = table[o, c]
            slot = slot + jnp.logical_and(held >= 0, held < wanted).astype(jnp.int32)
        return ref[jnp.minimum(slot, CAP - 1)], wanted >= 0

    def att_copy(order, i, kind):
        tile = odd + order * (1 - 2 * odd)
        slot = across if kind == 2 else head
        piece = att.at[slot, tile] if i is None else att.at[slot, tile, i]
        recv = att_recv.at[order, i if kind == 1 else n_bar + kind // 2]
        return pltpu.make_async_remote_copy(
            src_ref=piece, dst_ref=piece, send_sem=att_send, recv_sem=recv,
            device_id=(seq, across if kind == 1 else core), device_id_type=MESH,
        )

    def y_copy(i):
        return send(att_twin.at[i], att.at[head, odd, i], y_send, y_recv.at[i], (partner, head))

    def relay(order, i):
        att_copy(order, i, 1).wait_recv()
        att_copy(order, i, 2).start()

    @pl.when(has_outer)
    def _():
        pick_copy(0).wait_recv()

    @pl.when(has_inner)
    def _():
        near_all.wait_recv()

    last = n_bar - 1

    def band(mirror, i, beyond):
        blocks = [(mirror[n], None) for n in range(max(i - 1, 0), min(i + 2, n_bar))]
        if i == last:
            blocks.append((beyond[last], None))
        return blocks

    def own_first(i):
        b = slot_bar(i)
        blocks = band(own, i, twin)
        blocks.append(picked(bars, b, column(0, columns), pick_near))
        blocks.append(whole(bars, b, column(2, columns), twin, True))
        blocks.append(whole(bars, b, column(3, columns), near, False))
        return q_own[i], blocks, None

    def own_rest(i):
        blocks = [whole(bars, slot_bar(i), column(1, columns), back, True)]
        if i == 0:
            blocks.append((back[0], has_outer))
        return q_own[i], blocks, i

    def twin_bar(i):
        return last - i + odd * (2 * i - last)

    def twin_first(i):
        b = twin_bar(i)
        blocks = band(twin, i, own)
        if i == 0:
            blocks.append((near[0], has_inner))
        blocks.append(whole(twin_bars, b, column(0, columns), back, True))
        blocks.append(whole(twin_bars, b, column(1, columns), own, False))
        blocks.append(whole(twin_bars, b, column(2, columns), near, False))
        return q_twin[i], blocks, None

    def twin_rest(i):
        return q_twin[i], [picked(twin_bars, twin_bar(i), column(3, columns), pick_far)], n_bar + i

    slots = range(n_bar)
    keep(slots, weigh([own_first(i) for i in slots]))

    @pl.when(has_outer)
    def _():
        back_all.wait_recv()

    for i, state in zip(slots, weigh([own_rest(i) for i in slots])):
        att[head, odd, i] = finish(state)
    for i in slots:
        att_copy(0, i, 1).start()
        att_copy(0, i, 0).start()

    q_all.wait_recv()
    keep([n_bar + i for i in slots], weigh([twin_first(i) for i in slots]))

    @pl.when(has_inner)
    def _():
        pick_copy(1).wait_recv()

    for i, state in zip(slots, weigh([twin_rest(i) for i in slots])):
        att_twin[i] = finish(state)
    for i in slots:
        y_copy(i).start()

    def pass_on(i):
        y_copy(i).wait_recv()
        att_copy(1, i, 1).start()
        att_copy(1, i, 0).start()

    for i in range(last):
        relay(0, i)
    pass_on(0)
    relay(0, last)
    for i in range(1, n_bar):
        pass_on(i)

    own_w.wait()
    w_copy(0).wait_recv()
    w_copy(2).wait_recv()
    att_copy(0, None, 0).wait_recv()
    att_copy(0, None, 2).wait_recv()

    def out_copy(i):
        return pltpu.make_async_copy(out_ref.at[i], out_hbm.at[slot_bar(i)], out_sem)

    def project(tile, i):
        lhs = jnp.concatenate([att[m, tile, i] for m in range(n_head)], axis=1)
        at = pl.ds(pl.multiple_of(tile * LANES, LANES), LANES)
        rhs = jnp.concatenate([w_all[m, at, :] for m in range(n_head)], axis=0)
        return jnp.dot(lhs, rhs, preferred_element_type=jnp.float32)

    for i in range(n_bar):
        part[i] = project(odd, i)
        relay(1, i)
    att_copy(1, None, 0).wait_recv()
    att_copy(1, None, 2).wait_recv()
    for i in slots:
        out_ref[i] = (part[i] + project(other, i)).astype(jnp.bfloat16)
        out_copy(i).start()

    pltpu.make_async_copy(out_ref, out_hbm, out_sem).wait()
    bars_copy.wait_send()
    give_all.wait_send()
    q_all.wait_send()
    send(att_twin, att.at[head, odd], y_send, y_recv.at[0], (partner, head)).wait_send()
    for half in (att.at[0 : n_head - 1],):
        send(half, half, att_send, att_recv.at[0, 0], (seq, core)).wait_send()
    blocks = w_all.at[0:3]
    send(blocks, blocks, w_send, w_recv.at[0], (seq, core)).wait_send()

    @pl.when(has_outer)
    def _():
        near_all.wait_send()
        pick_copy(1).wait_send()

    @pl.when(has_inner)
    def _():
        back_all.wait_send()
        pick_copy(0).wait_send()


def solution(mesh):
    n_seq, n_head = mesh.shape["seq"], mesh.shape["head"]

    def on_device(queries, keys, values, masked, mask_qkv, key_bars, w_out):
        tokens, width = queries.shape
        bars, slots = key_bars.shape
        length = tokens // bars
        cols = w_out.shape[1] // n_head
        tiles = width // LANES
        shaped = [x.reshape(bars, length, width) for x in (queries, keys, values)]
        hbm = pl.BlockSpec(memory_space=pltpu.HBM)
        dma = pltpu.SemaphoreType.DMA
        bf16 = jnp.bfloat16
        pair = (bars, length, 2 * LANES)
        single = (bars, length, LANES)
        some = (CAP, length, 2 * LANES)
        out = pl.pallas_call(
            functools.partial(kernel, n_seq, n_head),
            out_shape=jax.ShapeDtypeStruct((bars, length, cols), bf16),
            in_specs=[hbm] * 7,
            out_specs=hbm,
            scratch_shapes=[
                pltpu.SMEM(key_bars.shape, jnp.int32),
                pltpu.SMEM(key_bars.shape, jnp.int32),
                pltpu.VMEM((bars, length), jnp.int32),
                pltpu.VMEM(mask_qkv.shape, bf16),
                pltpu.VMEM((3, bars, length, width), bf16),
            ]
            + [pltpu.VMEM(pair, bf16)] * 5
            + [pltpu.VMEM(some, bf16)] * 4
            + [pltpu.VMEM(single, bf16)] * 3
            + [
                pltpu.VMEM((n_head, width, cols), bf16),
                pltpu.VMEM((n_head, tiles, bars, length, LANES), bf16),
                pltpu.VMEM(single, bf16),
                pltpu.VMEM((bars, length, cols), jnp.float32),
                pltpu.VMEM((bars, length, cols), bf16),
            ]
            + [pltpu.VMEM((2 * bars, LANES // HD * length, LANES), jnp.float32)] * 3
            + [
                dma,
                dma((3,)),
                dma((3,)),
                dma,
                dma,
                dma,
                dma,
                dma((bars,)),
                dma,
                dma,
                dma,
                dma,
                dma,
                dma,
                dma((2,)),
                dma((2,)),
                dma,
                dma((3,)),
                dma,
                dma((bars,)),
                dma,
                dma((2, bars + 2)),
            ],
            compiler_params=pltpu.CompilerParams(
                collective_id=0, has_side_effects=True
            ),
            name="bar_attention",
        )(key_bars, masked.reshape(bars, length), mask_qkv, *shaped, w_out)
        return out.reshape(tokens, cols)

    placed = (
        P("seq", "head"),
        P("seq", "head"),
        P("seq", "head"),
        P("seq"),
        P(None, "head"),
        P("seq", None),
        P("head", None),
    )
    return jax.shard_map(
        on_device, mesh=mesh, in_specs=placed, out_specs=P("seq", "head"), check_vma=False
    )
```

```python
import functools

import jax
import jax.numpy as jnp
from jax import lax
from jax.experimental import pallas as pl
from jax.experimental.pallas import tpu as pltpu
from jax.sharding import PartitionSpec as P

HD = 64
CAP = 2
LANES = 128
MESH = pl.DeviceIdType.MESH
NEG = -1e30


def kernel(
    n_seq, n_head, bars_hbm, masked_hbm, mask_hbm, q_hbm, k_hbm, v_hbm, w_hbm, out_ref,
    bars, twin_bars, masked_ref, mask_ref, raw, own, give, twin, near, back, pack_own, pack_twin,
    pick_near, pick_far, q_own, q_give, q_twin, w_all, att, att_twin, part, acc, top, tot,
    small_sem, load_sem, w_own, bars_send, bars_recv, give_send, give_recv, q_send, q_recv,
    near_send, near_recv, back_send, back_recv, pick_send, pick_recv,
    w_send, w_recv, y_send, y_recv, att_send, att_recv, late_recv,
):
    seq = lax.axis_index("seq")
    head = lax.axis_index("head")
    n_bar, bar_len, out_cols = out_ref.shape
    odd = lax.rem(seq, 2)
    other = 1 - odd
    partner = seq + 1 - 2 * odd
    outer = seq - 2 + 4 * odd
    inner = seq + 2 - 4 * odd
    has_outer = jnp.logical_and(outer >= 0, outer < n_seq)
    has_inner = jnp.logical_and(inner >= 0, inner < n_seq)
    per_tile = LANES // HD

    def slot_bar(i):
        return i + odd * (n_bar - 1 - 2 * i)

    def column(c, count):
        return c + odd * (count - 1 - 2 * c)

    def column_twin(c, count):
        return column(c, count)

    columns = bars.shape[1]

    barrier = pltpu.get_barrier_semaphore()
    peers = [lax.rem(head + step, n_head) for step in range(1, n_head)]
    across = lax.rem(head + 2, n_head)
    count = n_head + 1
    for there, place in ((has_outer, outer), (has_inner, inner)):
        count = count + there.astype(jnp.int32)

        @pl.when(there)
        def _(place=place):
            pl.semaphore_signal(barrier, inc=1, device_id=(place, head), device_id_type=MESH)

    for place in (head, across):
        pl.semaphore_signal(barrier, inc=1, device_id=(partner, place), device_id_type=MESH)
    for peer in peers:
        pl.semaphore_signal(barrier, inc=1, device_id=(seq, peer), device_id_type=MESH)

    small = [
        pltpu.make_async_copy(source, target, small_sem.at[n])
        for n, (source, target) in enumerate(
            ((masked_hbm, masked_ref), (mask_hbm, mask_ref), (bars_hbm, bars))
        )
    ]
    for load in small:
        load.start()
    loads = [
        pltpu.make_async_copy(source, raw.at[n], load_sem.at[n])
        for n, source in enumerate((k_hbm, v_hbm, q_hbm))
    ]
    for load in loads:
        load.start()
    own_w = pltpu.make_async_copy(
        w_hbm.at[:, pl.ds(pl.multiple_of(head * out_cols, LANES), out_cols)], w_all.at[head], w_own
    )
    own_w.start()

    rows = lax.broadcasted_iota(jnp.int32, (bar_len, bar_len), 0)
    cols = lax.broadcasted_iota(jnp.int32, (bar_len, bar_len), 1)
    lane = lax.broadcasted_iota(jnp.int32, (bar_len, LANES), 1)
    mine = pl.ds(pl.multiple_of(odd * LANES, LANES), LANES)
    theirs = pl.ds(pl.multiple_of(other * LANES, LANES), LANES)

    for load in small:
        load.wait()
    hits = {}

    def flag(i):
        row = masked_ref[pl.ds(slot_bar(i), 1), :]
        hits[i] = jnp.max(jnp.where(rows == cols, row, 0), axis=1, keepdims=True) == 1

    def replaced(n, i, row, tile):
        mask_row = mask_ref[row : row + 1, tile].astype(jnp.float32)
        return jnp.where(hits[i], mask_row, raw[n, slot_bar(i), :, tile].astype(jnp.float32))

    def prepare(target, i, tile):
        target[i, :, :LANES] = replaced(0, i, 1, tile).astype(jnp.bfloat16)
        target[i, :, LANES:] = replaced(1, i, 2, tile).astype(jnp.bfloat16)

    def send(source, target, send_sem, recv_sem, place):
        return pltpu.make_async_remote_copy(
            src_ref=source, dst_ref=target, send_sem=send_sem, recv_sem=recv_sem,
            device_id=place, device_id_type=MESH,
        )

    def give_copy(i):
        return send(give.at[i], twin.at[i], give_send, give_recv.at[i], (partner, head))

    give_all = send(give, twin, give_send, give_recv.at[0], (partner, head))
    q_all = send(q_give, q_twin, q_send, q_recv, (partner, head))
    near_all = send(own, near, near_send, near_recv, (outer, head))
    back_all = send(twin, back, back_send, back_recv, (inner, head))

    def near_copy(i):
        return send(own.at[i], near.at[i], near_send, near_recv, (outer, head))

    def back_copy(i):
        return send(twin.at[i], back.at[i], back_send, back_recv, (inner, head))

    def pick_copy(far):
        if far:
            return send(pack_twin, pick_far, pick_send.at[1], pick_recv.at[1], (outer, head))
        return send(pack_own, pick_near, pick_send.at[0], pick_recv.at[0], (inner, head))

    bars_copy = pltpu.make_async_remote_copy(
        src_ref=bars_hbm, dst_ref=twin_bars, send_sem=bars_send, recv_sem=bars_recv,
        device_id=(partner, head), device_id_type=MESH,
    )

    core = head + 1 - 2 * lax.rem(head, 2)
    turn = lax.rem(seq // 2, 2)
    direct = across + turn * (1 - 2 * lax.rem(across, 2))
    mate = seq + 2 - 4 * turn

    def w_copy(step):
        if step == 2:
            source, target, place = w_all.at[direct], w_all.at[direct], (mate, head)
        else:
            peer = direct if step else core
            source = w_hbm.at[:, pl.ds(pl.multiple_of(peer * out_cols, LANES), out_cols)]
            target, place = w_all.at[head], (seq, peer)
        return send(source, target, w_send, w_recv.at[step], place)

    loads[0].wait()
    loads[1].wait()
    for i in range(n_bar):
        flag(i)
        prepare(give, i, theirs)
        prepare(own, i, mine)
        if i == 0:
            pl.semaphore_wait(barrier, count)
            bars_copy.start()
        give_copy(i).start()

        @pl.when(has_outer)
        def _(i=i):
            near_copy(i).start()

    for step in (1, 0):
        w_copy(step).start()

    def picks(table, c, turned):
        before = jnp.int32(0)
        chosen = [jnp.int32(0)] * CAP
        for b in range(n_bar):
            used = (table[b, c] >= 0).astype(jnp.int32)
            at = b + odd * (n_bar - 1 - 2 * b)
            if turned:
                at = n_bar - 1 - at
            for slot in range(CAP):
                chosen[slot] = chosen[slot] + jnp.where(before == slot, used * at, 0)
            before = before + used
        return chosen

    for slot, at in enumerate(picks(bars, column(columns - 1, columns), False)):
        pack_own[slot] = own[at]

    @pl.when(has_inner)
    def _():
        pick_copy(0).start()

    loads[2].wait()
    for i in range(n_bar):
        q_give[i] = (replaced(2, i, 0, theirs) * HD ** -0.5).astype(jnp.bfloat16)
    for i in range(n_bar):
        q_own[i] = (replaced(2, i, 0, mine) * HD ** -0.5).astype(jnp.bfloat16)

    @pl.when(jnp.logical_not(has_outer))
    def _():
        back[...] = jnp.zeros(back.shape, back.dtype)
        pick_near[...] = jnp.zeros(pick_near.shape, pick_near.dtype)

    @pl.when(jnp.logical_not(has_inner))
    def _():
        near[...] = jnp.zeros(near.shape, near.dtype)
        pick_far[...] = jnp.zeros(pick_far.shape, pick_far.dtype)

    for i in range(n_bar):
        give_copy(i).wait_recv()
        if i == 1:
            q_all.start()

        @pl.when(has_inner)
        def _(i=i):
            back_copy(i).start()

    bars_copy.wait_recv()
    for slot, at in enumerate(picks(twin_bars, column(0, columns), True)):
        pack_twin[slot] = twin[at]

    @pl.when(has_outer)
    def _():
        pick_copy(1).start()

    halves = [(lane // HD == h).astype(jnp.bfloat16) for h in range(per_tile)]

    def weigh(jobs):
        scores = []
        for query, blocks, _ in jobs:
            stacked = jnp.concatenate([query * half for half in halves], axis=0)
            row = []
            for block, usable in blocks:
                s = lax.dot_general(
                    stacked, block[:, :LANES], (((1,), (1,)), ((), ())), preferred_element_type=jnp.float32
                )
                if usable is not None:
                    s = s + jnp.where(usable, 0.0, NEG).astype(jnp.float32)
                row.append(s)
            scores.append(row)
        peaks, fades = [], []
        for row, (_, _, old) in zip(scores, jobs):
            peak = jnp.max(functools.reduce(jnp.maximum, row), axis=1, keepdims=True)
            if old is not None:
                peak = jnp.maximum(peak, top[old])
                fades.append(jnp.exp(top[old] - peak))
            else:
                fades.append(None)
            peaks.append(peak)
        totals, rounded = [], []
        for row, peak, fade, (_, _, old) in zip(scores, peaks, fades, jobs):
            raised = [jnp.exp(s - peak) for s in row]
            total = jnp.sum(functools.reduce(jnp.add, raised), axis=1, keepdims=True)
            if old is not None:
                total = total + tot[old] * fade
            totals.append(total)
            rounded.append(jnp.concatenate([r.astype(jnp.bfloat16) for r in raised], axis=1))
        sums = []
        for weight, fade, (_, blocks, old) in zip(rounded, fades, jobs):
            value = jnp.concatenate([block[:, LANES:] for block, _ in blocks], axis=0)
            weighted = jnp.dot(weight, value, preferred_element_type=jnp.float32)
            if old is not None:
                weighted = weighted + acc[old] * fade
            sums.append(weighted)
        return list(zip(peaks, totals, sums))

    def keep(slots, states):
        for slot, (peak, total, weighted) in zip(slots, states):
            top[slot] = jnp.broadcast_to(peak, top.shape[1:])
            tot[slot] = jnp.broadcast_to(total, tot.shape[1:])
            acc[slot] = weighted

    def finish(state):
        _, total, weighted = state
        done = weighted / total
        result = done[:bar_len]
        for h in range(1, per_tile):
            result = jnp.where(lane // HD == h, done[h * bar_len : (h + 1) * bar_len], result)
        return result.astype(jnp.bfloat16)

    def whole(table, b, c, ref, turned):
        wanted = table[b, c]
        at = lax.rem(jnp.maximum(wanted, 0), n_bar)
        at = at + odd * (n_bar - 1 - 2 * at)
        if turned:
            at = n_bar - 1 - at
        return ref[at], wanted >= 0

    def picked(table, b, c, ref):
        wanted = table[b, c]
        slot = jnp.int32(0)
        for o in range(n_bar):
            held = table[o, c]
            slot = slot + jnp.logical_and(held >= 0, held < wanted).astype(jnp.int32)
        return ref[jnp.minimum(slot, CAP - 1)], wanted >= 0

    def att_copy(order, i, kind):
        tile = odd + order * (1 - 2 * odd)
        slot = across if kind == 2 else head
        piece = att.at[slot, tile] if i is None else att.at[slot, tile, i]
        if order and kind != 1:
            recv = late_recv.at[i, kind // 2]
        else:
            recv = att_recv.at[order, i if kind == 1 else n_bar + kind // 2]
        return pltpu.make_async_remote_copy(
            src_ref=piece, dst_ref=piece, send_sem=att_send, recv_sem=recv,
            device_id=(seq, across if kind == 1 else core), device_id_type=MESH,
        )

    def y_copy(i):
        return send(att_twin.at[i], att.at[head, odd, i], y_send, y_recv.at[i], (partner, head))

    def corner_copy(i):
        return send(att_twin.at[i], att.at[head, odd, i], att_send, att_recv.at[1, i], (partner, across))

    def relay(order, i):
        att_copy(order, i, 1).wait_recv()
        att_copy(order, i, 2).start()

    @pl.when(has_outer)
    def _():
        pick_copy(0).wait_recv()

    @pl.when(has_inner)
    def _():
        near_all.wait_recv()

    last = n_bar - 1

    def band(mirror, i, beyond):
        blocks = [(mirror[n], None) for n in range(max(i - 1, 0), min(i + 2, n_bar))]
        if i == last:
            blocks.append((beyond[last], None))
        return blocks

    def own_first(i):
        b = slot_bar(i)
        blocks = band(own, i, twin)
        blocks.append(picked(bars, b, column(0, columns), pick_near))
        blocks.append(whole(bars, b, column(2, columns), twin, True))
        blocks.append(whole(bars, b, column(3, columns), near, False))
        return q_own[i], blocks, None

    def own_rest(i):
        blocks = [whole(bars, slot_bar(i), column(1, columns), back, True)]
        if i == 0:
            blocks.append((back[0], has_outer))
        return q_own[i], blocks, i

    def twin_bar(i):
        return last - i + odd * (2 * i - last)

    def twin_first(i):
        b = twin_bar(i)
        blocks = band(twin, i, own)
        if i == 0:
            blocks.append((near[0], has_inner))
        blocks.append(whole(twin_bars, b, column(1, columns), own, False))
        blocks.append(whole(twin_bars, b, column(2, columns), near, False))
        return q_twin[i], blocks, None

    def twin_rest(i):
        b = twin_bar(i)
        blocks = [whole(twin_bars, b, column(0, columns), back, True)]
        blocks.append(picked(twin_bars, b, column(3, columns), pick_far))
        return q_twin[i], blocks, n_bar + i

    slots = range(n_bar)
    keep(slots, weigh([own_first(i) for i in slots]))

    q_all.wait_recv()
    keep([n_bar + i for i in slots], weigh([twin_first(i) for i in slots]))

    @pl.when(has_outer)
    def _():
        back_all.wait_recv()

    for i, state in zip(slots, weigh([own_rest(i) for i in slots])):
        att[head, odd, i] = finish(state)
    for i in slots:
        att_copy(0, i, 1).start()
        att_copy(0, i, 0).start()
    w_copy(1).wait_recv()
    w_copy(2).start()

    @pl.when(has_inner)
    def _():
        pick_copy(1).wait_recv()

    for i, state in zip(slots, weigh([twin_rest(i) for i in slots])):
        att_twin[i] = finish(state)
    for i in slots:
        corner_copy(i).start()
        y_copy(i).start()
    for i in slots:
        relay(0, i)
    for i in slots:
        y_copy(i).wait_recv()
        att_copy(1, i, 0).start()
        relay(1, i)

    own_w.wait()
    w_copy(0).wait_recv()
    w_copy(2).wait_recv()
    att_copy(0, None, 0).wait_recv()
    att_copy(0, None, 2).wait_recv()

    def project(members, tile, lhs_of):
        lhs = jnp.concatenate([lhs_of(m, tile) for m in members], axis=1)
        at = pl.ds(pl.multiple_of(tile * LANES, LANES), LANES)
        rhs = jnp.concatenate([w_all[m, at, :] for m in members], axis=0)
        return jnp.dot(lhs, rhs, preferred_element_type=jnp.float32)

    def all_bars(m, tile):
        return att[m, tile].reshape(n_bar * bar_len, LANES)

    beside = across + 1 - 2 * lax.rem(across, 2)
    part[...] = project(range(n_head), odd, all_bars)
    part[...] += project((head, across), other, all_bars)
    for i in slots:
        att_copy(1, i, 0).wait_recv()
        att_copy(1, i, 2).wait_recv()
        rest = project((core, beside), other, lambda m, tile: att[m, tile, i])
        out_ref[slot_bar(i)] = (part[i * bar_len : (i + 1) * bar_len] + rest).astype(jnp.bfloat16)

    bars_copy.wait_send()
    give_all.wait_send()
    q_all.wait_send()
    send(att_twin, att.at[head, odd], y_send, y_recv.at[0], (partner, head)).wait_send()
    sent = att.at[0 : n_head - 1]
    send(sent, sent, att_send, att_recv.at[0, 0], (seq, core)).wait_send()
    blocks = w_all.at[0:3]
    send(blocks, blocks, w_send, w_recv.at[0], (seq, core)).wait_send()

    @pl.when(has_outer)
    def _():
        near_all.wait_send()
        pick_copy(1).wait_send()

    @pl.when(has_inner)
    def _():
        back_all.wait_send()
        pick_copy(0).wait_send()


def solution(mesh):
    n_seq, n_head = mesh.shape["seq"], mesh.shape["head"]

    def on_device(queries, keys, values, masked, mask_qkv, key_bars, w_out):
        tokens, width = queries.shape
        bars, slots = key_bars.shape
        length = tokens // bars
        cols = w_out.shape[1] // n_head
        tiles = width // LANES
        shaped = [x.reshape(bars, length, width) for x in (queries, keys, values)]
        hbm = pl.BlockSpec(memory_space=pltpu.HBM)
        dma = pltpu.SemaphoreType.DMA
        bf16 = jnp.bfloat16
        pair = (bars, length, 2 * LANES)
        single = (bars, length, LANES)
        some = (CAP, length, 2 * LANES)
        out = pl.pallas_call(
            functools.partial(kernel, n_seq, n_head),
            out_shape=pltpu.VMEM((bars, length, cols), bf16),
            in_specs=[hbm] * 7,
            out_specs=pl.BlockSpec(memory_space=pltpu.VMEM),
            scratch_shapes=[
                pltpu.SMEM(key_bars.shape, jnp.int32),
                pltpu.SMEM(key_bars.shape, jnp.int32),
                pltpu.VMEM((bars, length), jnp.int32),
                pltpu.VMEM(mask_qkv.shape, bf16),
                pltpu.VMEM((3, bars, length, width), bf16),
            ]
            + [pltpu.VMEM(pair, bf16)] * 5
            + [pltpu.VMEM(some, bf16)] * 4
            + [pltpu.VMEM(single, bf16)] * 3
            + [
                pltpu.VMEM((n_head, width, cols), bf16),
                pltpu.VMEM((n_head, tiles, bars, length, LANES), bf16),
                pltpu.VMEM(single, bf16),
                pltpu.VMEM((tokens, cols), jnp.float32),
            ]
            + [pltpu.VMEM((2 * bars, LANES // HD * length, LANES), jnp.float32)] * 3
            + [
                dma((3,)),
                dma((3,)),
                dma,
                dma,
                dma,
                dma,
                dma((bars,)),
                dma,
                dma,
                dma,
                dma,
                dma,
                dma,
                dma((2,)),
                dma((2,)),
                dma,
                dma((3,)),
                dma,
                dma((bars,)),
                dma,
                dma((2, bars + 2)),
                dma((bars, 2)),
            ],
            compiler_params=pltpu.CompilerParams(
                collective_id=0, has_side_effects=True, vmem_limit_bytes=40 * 1024 * 1024
            ),
            name="bar_attention",
        )(*(pltpu.with_memory_space_constraint(x, pltpu.HBM) for x in (key_bars, masked.reshape(bars, length), mask_qkv, *shaped, w_out)))
        return out.reshape(tokens, cols)

    placed = (
        P("seq", "head"),
        P("seq", "head"),
        P("seq", "head"),
        P("seq"),
        P(None, "head"),
        P("seq", None),
        P("head", None),
    )
    return jax.shard_map(
        on_device, mesh=mesh, in_specs=placed, out_specs=P("seq", "head"), check_vma=False
    )
```

```python
import functools

import jax
import jax.numpy as jnp
from jax import lax
from jax.experimental import pallas as pl
from jax.experimental.pallas import tpu as pltpu
from jax.sharding import PartitionSpec as P

HD = 64
CAP = 2
GROUP = 2
LANES = 128
MESH = pl.DeviceIdType.MESH
NEG = -1e30


def kernel(
    n_seq, n_head, bars_hbm, masked_hbm, mask_hbm, q_hbm, k_hbm, v_hbm, w_hbm, out_ref,
    bars, twin_bars, masked_ref, mask_ref, raw, own, give, twin, near, back, pack_own, pack_twin,
    pick_near, pick_far, q_own, q_give, q_twin, w_all, att, att_twin, part, acc, top, tot,
    small_sem, load_sem, w_own, bars_send, bars_recv, give_send, give_recv, q_send, q_recv,
    near_send, near_recv, back_send, back_recv, pick_send, pick_recv,
    w_send, w_recv, y_send, y_recv, att_send, att_recv, late_recv,
):
    seq = lax.axis_index("seq")
    head = lax.axis_index("head")
    n_bar, bar_len, out_cols = out_ref.shape
    odd = lax.rem(seq, 2)
    other = 1 - odd
    partner = seq + 1 - 2 * odd
    outer = seq - 2 + 4 * odd
    inner = seq + 2 - 4 * odd
    has_outer = jnp.logical_and(outer >= 0, outer < n_seq)
    has_inner = jnp.logical_and(inner >= 0, inner < n_seq)
    per_tile = LANES // HD

    def slot_bar(i):
        return i + odd * (n_bar - 1 - 2 * i)

    def column(c, count):
        return c + odd * (count - 1 - 2 * c)

    def column_twin(c, count):
        return column(c, count)

    columns = bars.shape[1]

    barrier = pltpu.get_barrier_semaphore()
    peers = [lax.rem(head + step, n_head) for step in range(1, n_head)]
    across = lax.rem(head + 2, n_head)
    count = n_head + 1
    for there, place in ((has_outer, outer), (has_inner, inner)):
        count = count + there.astype(jnp.int32)

        @pl.when(there)
        def _(place=place):
            pl.semaphore_signal(barrier, inc=1, device_id=(place, head), device_id_type=MESH)

    for place in (head, across):
        pl.semaphore_signal(barrier, inc=1, device_id=(partner, place), device_id_type=MESH)
    for peer in peers:
        pl.semaphore_signal(barrier, inc=1, device_id=(seq, peer), device_id_type=MESH)

    small = [
        pltpu.make_async_copy(source, target, small_sem.at[n])
        for n, (source, target) in enumerate(
            ((masked_hbm, masked_ref), (mask_hbm, mask_ref), (bars_hbm, bars))
        )
    ]
    for load in small:
        load.start()
    loads = [
        pltpu.make_async_copy(source, raw.at[n], load_sem.at[n])
        for n, source in enumerate((k_hbm, v_hbm, q_hbm))
    ]
    for load in loads:
        load.start()
    own_w = pltpu.make_async_copy(
        w_hbm.at[:, pl.ds(pl.multiple_of(head * out_cols, LANES), out_cols)], w_all.at[head], w_own
    )
    own_w.start()

    rows = lax.broadcasted_iota(jnp.int32, (bar_len, bar_len), 0)
    cols = lax.broadcasted_iota(jnp.int32, (bar_len, bar_len), 1)
    lane = lax.broadcasted_iota(jnp.int32, (bar_len, LANES), 1)
    mine = pl.ds(pl.multiple_of(odd * LANES, LANES), LANES)
    theirs = pl.ds(pl.multiple_of(other * LANES, LANES), LANES)

    for load in small:
        load.wait()
    hits = {}

    def flag(i):
        row = masked_ref[pl.ds(slot_bar(i), 1), :]
        hits[i] = jnp.max(jnp.where(rows == cols, row, 0), axis=1, keepdims=True) == 1

    def replaced(n, i, row, tile):
        mask_row = mask_ref[row : row + 1, tile].astype(jnp.float32)
        return jnp.where(hits[i], mask_row, raw[n, slot_bar(i), :, tile].astype(jnp.float32))

    def prepare(target, i, tile):
        target[i, :, :LANES] = replaced(0, i, 1, tile).astype(jnp.bfloat16)
        target[i, :, LANES:] = replaced(1, i, 2, tile).astype(jnp.bfloat16)

    def send(source, target, send_sem, recv_sem, place):
        return pltpu.make_async_remote_copy(
            src_ref=source, dst_ref=target, send_sem=send_sem, recv_sem=recv_sem,
            device_id=place, device_id_type=MESH,
        )

    def give_copy(i):
        return send(give.at[i], twin.at[i], give_send, give_recv.at[i], (partner, head))

    give_all = send(give, twin, give_send, give_recv.at[0], (partner, head))
    q_all = send(q_give, q_twin, q_send, q_recv, (partner, head))
    near_all = send(own, near, near_send, near_recv, (outer, head))
    back_all = send(twin, back, back_send, back_recv, (inner, head))

    def near_copy(i):
        return send(own.at[i], near.at[i], near_send, near_recv, (outer, head))

    def back_copy(i):
        return send(twin.at[i], back.at[i], back_send, back_recv, (inner, head))

    def pick_copy(far):
        if far:
            return send(pack_twin, pick_far, pick_send.at[1], pick_recv.at[1], (outer, head))
        return send(pack_own, pick_near, pick_send.at[0], pick_recv.at[0], (inner, head))

    bars_copy = pltpu.make_async_remote_copy(
        src_ref=bars_hbm, dst_ref=twin_bars, send_sem=bars_send, recv_sem=bars_recv,
        device_id=(partner, head), device_id_type=MESH,
    )

    core = head + 1 - 2 * lax.rem(head, 2)
    turn = lax.rem(seq // 2, 2)
    direct = across + turn * (1 - 2 * lax.rem(across, 2))
    mate = seq + 2 - 4 * turn

    def w_copy(step):
        if step == 2:
            source, target, place = w_all.at[direct], w_all.at[direct], (mate, head)
        else:
            peer = direct if step else core
            source = w_hbm.at[:, pl.ds(pl.multiple_of(peer * out_cols, LANES), out_cols)]
            target, place = w_all.at[head], (seq, peer)
        return send(source, target, w_send, w_recv.at[step], place)

    loads[0].wait()
    loads[1].wait()
    for i in range(n_bar):
        flag(i)
        prepare(give, i, theirs)
        prepare(own, i, mine)
        if i == 0:
            pl.semaphore_wait(barrier, count)
            bars_copy.start()
        give_copy(i).start()

        @pl.when(has_outer)
        def _(i=i):
            near_copy(i).start()

    for step in (1, 0):
        w_copy(step).start()

    def picks(table, c, turned):
        before = jnp.int32(0)
        chosen = [jnp.int32(0)] * CAP
        for b in range(n_bar):
            used = (table[b, c] >= 0).astype(jnp.int32)
            at = b + odd * (n_bar - 1 - 2 * b)
            if turned:
                at = n_bar - 1 - at
            for slot in range(CAP):
                chosen[slot] = chosen[slot] + jnp.where(before == slot, used * at, 0)
            before = before + used
        return chosen

    for slot, at in enumerate(picks(bars, column(columns - 1, columns), False)):
        pack_own[slot] = own[at]

    @pl.when(has_inner)
    def _():
        pick_copy(0).start()

    loads[2].wait()
    for i in range(n_bar):
        q_give[i] = (replaced(2, i, 0, theirs) * HD ** -0.5).astype(jnp.bfloat16)
    for i in range(n_bar):
        q_own[i] = (replaced(2, i, 0, mine) * HD ** -0.5).astype(jnp.bfloat16)

    @pl.when(jnp.logical_not(has_outer))
    def _():
        back[...] = jnp.zeros(back.shape, back.dtype)
        pick_near[...] = jnp.zeros(pick_near.shape, pick_near.dtype)

    @pl.when(jnp.logical_not(has_inner))
    def _():
        near[...] = jnp.zeros(near.shape, near.dtype)
        pick_far[...] = jnp.zeros(pick_far.shape, pick_far.dtype)

    for i in range(n_bar):
        give_copy(i).wait_recv()
        if i == 1:
            q_all.start()

        @pl.when(has_inner)
        def _(i=i):
            back_copy(i).start()

    bars_copy.wait_recv()
    for slot, at in enumerate(picks(twin_bars, column(0, columns), True)):
        pack_twin[slot] = twin[at]

    @pl.when(has_outer)
    def _():
        pick_copy(1).start()

    halves = [(lane // HD == h).astype(jnp.bfloat16) for h in range(per_tile)]

    def weigh(jobs):
        scores = []
        for query, blocks, _ in jobs:
            stacked = jnp.concatenate([query * half for half in halves], axis=0)
            row = []
            for block, usable in blocks:
                s = lax.dot_general(
                    stacked, block[:, :LANES], (((1,), (1,)), ((), ())), preferred_element_type=jnp.float32
                )
                if usable is not None:
                    s = s + jnp.where(usable, 0.0, NEG).astype(jnp.float32)
                row.append(s)
            scores.append(row)
        peaks, fades = [], []
        for row, (_, _, old) in zip(scores, jobs):
            peak = jnp.max(functools.reduce(jnp.maximum, row), axis=1, keepdims=True)
            if old is not None:
                peak = jnp.maximum(peak, top[old])
                fades.append(jnp.exp(top[old] - peak))
            else:
                fades.append(None)
            peaks.append(peak)
        totals, rounded = [], []
        for row, peak, fade, (_, _, old) in zip(scores, peaks, fades, jobs):
            raised = [jnp.exp(s - peak) for s in row]
            total = jnp.sum(functools.reduce(jnp.add, raised), axis=1, keepdims=True)
            if old is not None:
                total = total + tot[old] * fade
            totals.append(total)
            rounded.append(jnp.concatenate([r.astype(jnp.bfloat16) for r in raised], axis=1))
        sums = []
        for weight, fade, (_, blocks, old) in zip(rounded, fades, jobs):
            value = jnp.concatenate([block[:, LANES:] for block, _ in blocks], axis=0)
            weighted = jnp.dot(weight, value, preferred_element_type=jnp.float32)
            if old is not None:
                weighted = weighted + acc[old] * fade
            sums.append(weighted)
        return list(zip(peaks, totals, sums))

    def keep(slots, states):
        for slot, (peak, total, weighted) in zip(slots, states):
            top[slot] = jnp.broadcast_to(peak, top.shape[1:])
            tot[slot] = jnp.broadcast_to(total, tot.shape[1:])
            acc[slot] = weighted

    def finish(state):
        _, total, weighted = state
        done = weighted / total
        result = done[:bar_len]
        for h in range(1, per_tile):
            result = jnp.where(lane // HD == h, done[h * bar_len : (h + 1) * bar_len], result)
        return result.astype(jnp.bfloat16)

    def whole(table, b, c, ref, turned):
        wanted = table[b, c]
        at = lax.rem(jnp.maximum(wanted, 0), n_bar)
        at = at + odd * (n_bar - 1 - 2 * at)
        if turned:
            at = n_bar - 1 - at
        return ref[at], wanted >= 0

    def picked(table, b, c, ref):
        wanted = table[b, c]
        slot = jnp.int32(0)
        for o in range(n_bar):
            held = table[o, c]
            slot = slot + jnp.logical_and(held >= 0, held < wanted).astype(jnp.int32)
        return ref[jnp.minimum(slot, CAP - 1)], wanted >= 0

    def att_copy(order, i, kind):
        tile = odd + order * (1 - 2 * odd)
        slot = across if kind == 2 else head
        piece = att.at[slot, tile] if i is None else att.at[slot, tile, i]
        if order and kind != 1:
            recv = late_recv.at[i, kind // 2]
        else:
            recv = att_recv.at[order, i if kind == 1 else n_bar + kind // 2]
        return pltpu.make_async_remote_copy(
            src_ref=piece, dst_ref=piece, send_sem=att_send, recv_sem=recv,
            device_id=(seq, across if kind == 1 else core), device_id_type=MESH,
        )

    def y_copy(i):
        return send(att_twin.at[i], att.at[head, odd, i], y_send, y_recv.at[i], (partner, head))

    def corner_copy(i):
        return send(att_twin.at[i], att.at[head, odd, i], att_send, att_recv.at[1, i], (partner, across))

    def relay(order, i):
        att_copy(order, i, 1).wait_recv()
        att_copy(order, i, 2).start()

    @pl.when(has_outer)
    def _():
        pick_copy(0).wait_recv()

    @pl.when(has_inner)
    def _():
        near_all.wait_recv()

    last = n_bar - 1

    def band(mirror, i, beyond):
        blocks = [(mirror[n], None) for n in range(max(i - 1, 0), min(i + 2, n_bar))]
        if i == last:
            blocks.append((beyond[last], None))
        return blocks

    def own_first(i):
        b = slot_bar(i)
        blocks = band(own, i, twin)
        blocks.append(picked(bars, b, column(0, columns), pick_near))
        blocks.append(whole(bars, b, column(2, columns), twin, True))
        blocks.append(whole(bars, b, column(3, columns), near, False))
        return q_own[i], blocks, None

    def own_rest(i):
        blocks = [whole(bars, slot_bar(i), column(1, columns), back, True)]
        if i == 0:
            blocks.append((back[0], has_outer))
        return q_own[i], blocks, i

    def twin_bar(i):
        return last - i + odd * (2 * i - last)

    def twin_first(i):
        b = twin_bar(i)
        blocks = band(twin, i, own)
        if i == 0:
            blocks.append((near[0], has_inner))
        blocks.append(whole(twin_bars, b, column(1, columns), own, False))
        blocks.append(whole(twin_bars, b, column(2, columns), near, False))
        return q_twin[i], blocks, None

    def twin_rest(i):
        b = twin_bar(i)
        blocks = [whole(twin_bars, b, column(0, columns), back, True)]
        blocks.append(picked(twin_bars, b, column(3, columns), pick_far))
        return q_twin[i], blocks, n_bar + i

    slots = range(n_bar)
    keep(slots, weigh([own_first(i) for i in slots]))

    q_all.wait_recv()
    keep([n_bar + i for i in slots], weigh([twin_first(i) for i in slots]))

    @pl.when(has_outer)
    def _():
        back_all.wait_recv()

    def finish_own():
        for i, state in zip(slots, weigh([own_rest(i) for i in slots])):
            att[head, odd, i] = finish(state)
        for i in slots:
            att_copy(0, i, 1).start()
            att_copy(0, i, 0).start()

    pl.when(odd == 0)(finish_own)

    @pl.when(has_inner)
    def _():
        pick_copy(1).wait_recv()

    for i, state in zip(slots, weigh([twin_rest(i) for i in slots])):
        att_twin[i] = finish(state)
    for i in slots:
        corner_copy(i).start()
        y_copy(i).start()

    pl.when(odd == 1)(finish_own)
    w_copy(1).wait_recv()
    w_copy(2).start()

    for i in slots:
        relay(0, i)
    def project(members, tile, span):
        lhs = jnp.concatenate([att[m, tile, span].reshape(-1, LANES) for m in members], axis=1)
        at = pl.ds(pl.multiple_of(tile * LANES, LANES), LANES)
        rhs = jnp.concatenate([w_all[m, at, :] for m in members], axis=0)
        return jnp.dot(lhs, rhs, preferred_element_type=jnp.float32)

    def forward(i):
        y_copy(i).wait_recv()
        att_copy(1, i, 0).start()
        relay(1, i)

    near_side, far_side = (head, across), (core, across + 1 - 2 * lax.rem(across, 2))
    every = slice(0, n_bar)
    for i in slots[: n_bar // 2]:
        forward(i)
    own_w.wait()
    w_copy(0).wait_recv()
    w_copy(2).wait_recv()
    part[...] = project(near_side, odd, every)
    for i in slots[n_bar // 2 :]:
        forward(i)
    part[...] += project(near_side, other, every)
    att_copy(0, None, 0).wait_recv()
    att_copy(0, None, 2).wait_recv()
    part[...] += project(far_side, odd, every)
    for g in range(0, n_bar, GROUP):
        for i in slots[g : g + GROUP]:
            att_copy(1, i, 0).wait_recv()
            att_copy(1, i, 2).wait_recv()
        rest = project(far_side, other, slice(g, g + GROUP))
        for i in slots[g : g + GROUP]:
            row = (i - g) * bar_len
            whole_bar = part[i * bar_len : (i + 1) * bar_len] + rest[row : row + bar_len]
            out_ref[slot_bar(i)] = whole_bar.astype(jnp.bfloat16)

    bars_copy.wait_send()
    give_all.wait_send()
    q_all.wait_send()
    send(att_twin, att.at[head, odd], y_send, y_recv.at[0], (partner, head)).wait_send()
    sent = att.at[0 : n_head - 1]
    send(sent, sent, att_send, att_recv.at[0, 0], (seq, core)).wait_send()
    blocks = w_all.at[0:3]
    send(blocks, blocks, w_send, w_recv.at[0], (seq, core)).wait_send()

    @pl.when(has_outer)
    def _():
        near_all.wait_send()
        pick_copy(1).wait_send()

    @pl.when(has_inner)
    def _():
        back_all.wait_send()
        pick_copy(0).wait_send()


def solution(mesh):
    n_seq, n_head = mesh.shape["seq"], mesh.shape["head"]

    def on_device(queries, keys, values, masked, mask_qkv, key_bars, w_out):
        tokens, width = queries.shape
        bars, slots = key_bars.shape
        length = tokens // bars
        cols = w_out.shape[1] // n_head
        tiles = width // LANES
        shaped = [x.reshape(bars, length, width) for x in (queries, keys, values)]
        hbm = pl.BlockSpec(memory_space=pltpu.HBM)
        dma = pltpu.SemaphoreType.DMA
        bf16 = jnp.bfloat16
        pair = (bars, length, 2 * LANES)
        single = (bars, length, LANES)
        some = (CAP, length, 2 * LANES)
        out = pl.pallas_call(
            functools.partial(kernel, n_seq, n_head),
            out_shape=pltpu.VMEM((bars, length, cols), bf16),
            in_specs=[hbm] * 7,
            out_specs=pl.BlockSpec(memory_space=pltpu.VMEM),
            scratch_shapes=[
                pltpu.SMEM(key_bars.shape, jnp.int32),
                pltpu.SMEM(key_bars.shape, jnp.int32),
                pltpu.VMEM((bars, length), jnp.int32),
                pltpu.VMEM(mask_qkv.shape, bf16),
                pltpu.VMEM((3, bars, length, width), bf16),
            ]
            + [pltpu.VMEM(pair, bf16)] * 5
            + [pltpu.VMEM(some, bf16)] * 4
            + [pltpu.VMEM(single, bf16)] * 3
            + [
                pltpu.VMEM((n_head, width, cols), bf16),
                pltpu.VMEM((n_head, tiles, bars, length, LANES), bf16),
                pltpu.VMEM(single, bf16),
                pltpu.VMEM((tokens, cols), jnp.float32),
            ]
            + [pltpu.VMEM((2 * bars, LANES // HD * length, LANES), jnp.float32)] * 3
            + [
                dma((3,)),
                dma((3,)),
                dma,
                dma,
                dma,
                dma,
                dma((bars,)),
                dma,
                dma,
                dma,
                dma,
                dma,
                dma,
                dma((2,)),
                dma((2,)),
                dma,
                dma((3,)),
                dma,
                dma((bars,)),
                dma,
                dma((2, bars + 2)),
                dma((bars, 2)),
            ],
            compiler_params=pltpu.CompilerParams(
                collective_id=0, has_side_effects=True, vmem_limit_bytes=40 * 1024 * 1024
            ),
            name="bar_attention",
        )(*(pltpu.with_memory_space_constraint(x, pltpu.HBM) for x in (key_bars, masked.reshape(bars, length), mask_qkv, *shaped, w_out)))
        return out.reshape(tokens, cols)

    placed = (
        P("seq", "head"),
        P("seq", "head"),
        P("seq", "head"),
        P("seq"),
        P(None, "head"),
        P("seq", None),
        P("head", None),
    )
    return jax.shard_map(
        on_device, mesh=mesh, in_specs=placed, out_specs=P("seq", "head"), check_vma=False
    )
```

```python
import functools

import jax
import jax.numpy as jnp
from jax import lax
from jax.experimental import pallas as pl
from jax.experimental.pallas import tpu as pltpu
from jax.sharding import PartitionSpec as P

HD = 64
CAP = 2
GROUP = 2
LANES = 128
MESH = pl.DeviceIdType.MESH
NEG = -1e30


def kernel(
    n_seq, n_head, bars_hbm, masked_hbm, mask_hbm, q_hbm, k_hbm, v_hbm, w_hbm, out_ref,
    bars, twin_bars, masked_ref, mask_ref, raw, own, give, twin, near, back, pack_own, pack_twin,
    pick_near, pick_far, q_own, q_give, q_twin, w_all, att, att_twin, part, acc, top, tot,
    small_sem, load_sem, w_own, bars_send, bars_recv, give_send, give_recv, q_send, q_recv,
    near_send, near_recv, back_send, back_recv, pick_send, pick_recv,
    w_send, w_recv, y_send, y_recv, att_send, att_recv, late_recv,
):
    seq = lax.axis_index("seq")
    head = lax.axis_index("head")
    n_bar, bar_len, out_cols = out_ref.shape
    odd = lax.rem(seq, 2)
    other = 1 - odd
    partner = seq + 1 - 2 * odd
    outer = seq - 2 + 4 * odd
    inner = seq + 2 - 4 * odd
    has_outer = jnp.logical_and(outer >= 0, outer < n_seq)
    has_inner = jnp.logical_and(inner >= 0, inner < n_seq)
    per_tile = LANES // HD

    def slot_bar(i):
        return i + odd * (n_bar - 1 - 2 * i)

    def column(c, count):
        return c + odd * (count - 1 - 2 * c)

    def column_twin(c, count):
        return column(c, count)

    columns = bars.shape[1]

    barrier = pltpu.get_barrier_semaphore()
    peers = [lax.rem(head + step, n_head) for step in range(1, n_head)]
    across = lax.rem(head + 2, n_head)
    count = n_head + 1
    for there, place in ((has_outer, outer), (has_inner, inner)):
        count = count + there.astype(jnp.int32)

        @pl.when(there)
        def _(place=place):
            pl.semaphore_signal(barrier, inc=1, device_id=(place, head), device_id_type=MESH)

    for place in (head, across):
        pl.semaphore_signal(barrier, inc=1, device_id=(partner, place), device_id_type=MESH)
    for peer in peers:
        pl.semaphore_signal(barrier, inc=1, device_id=(seq, peer), device_id_type=MESH)

    small = [
        pltpu.make_async_copy(source, target, small_sem.at[n])
        for n, (source, target) in enumerate(
            ((masked_hbm, masked_ref), (mask_hbm, mask_ref), (bars_hbm, bars))
        )
    ]
    for load in small:
        load.start()
    loads = [
        pltpu.make_async_copy(source, raw.at[n], load_sem.at[n])
        for n, source in enumerate((k_hbm, v_hbm, q_hbm))
    ]
    for load in loads:
        load.start()
    own_w = pltpu.make_async_copy(
        w_hbm.at[:, pl.ds(pl.multiple_of(head * out_cols, LANES), out_cols)], w_all.at[head], w_own
    )
    own_w.start()

    rows = lax.broadcasted_iota(jnp.int32, (bar_len, bar_len), 0)
    cols = lax.broadcasted_iota(jnp.int32, (bar_len, bar_len), 1)
    lane = lax.broadcasted_iota(jnp.int32, (bar_len, LANES), 1)
    mine = pl.ds(pl.multiple_of(odd * LANES, LANES), LANES)
    theirs = pl.ds(pl.multiple_of(other * LANES, LANES), LANES)

    for load in small:
        load.wait()
    hits = {}

    def flag(i):
        row = masked_ref[pl.ds(slot_bar(i), 1), :]
        hits[i] = jnp.max(jnp.where(rows == cols, row, 0), axis=1, keepdims=True) == 1

    def replaced(n, i, row, tile):
        mask_row = mask_ref[row : row + 1, tile].astype(jnp.float32)
        return jnp.where(hits[i], mask_row, raw[n, slot_bar(i), :, tile].astype(jnp.float32))

    def prepare(target, i, tile):
        target[i, :, :LANES] = replaced(0, i, 1, tile).astype(jnp.bfloat16)
        target[i, :, LANES:] = replaced(1, i, 2, tile).astype(jnp.bfloat16)

    def send(source, target, send_sem, recv_sem, place):
        return pltpu.make_async_remote_copy(
            src_ref=source, dst_ref=target, send_sem=send_sem, recv_sem=recv_sem,
            device_id=place, device_id_type=MESH,
        )

    def give_copy(i):
        return send(give.at[i], twin.at[i], give_send, give_recv.at[i], (partner, head))

    give_all = send(give, twin, give_send, give_recv.at[0], (partner, head))
    q_all = send(q_give, q_twin, q_send, q_recv, (partner, head))
    near_all = send(own, near, near_send, near_recv, (outer, head))
    back_all = send(twin, back, back_send, back_recv, (inner, head))

    def near_copy(i):
        return send(own.at[i], near.at[i], near_send, near_recv, (outer, head))

    def back_copy(i):
        return send(twin.at[i], back.at[i], back_send, back_recv, (inner, head))

    def pick_copy(far):
        if far:
            return send(pack_twin, pick_far, pick_send.at[1], pick_recv.at[1], (outer, head))
        return send(pack_own, pick_near, pick_send.at[0], pick_recv.at[0], (inner, head))

    bars_copy = pltpu.make_async_remote_copy(
        src_ref=bars_hbm, dst_ref=twin_bars, send_sem=bars_send, recv_sem=bars_recv,
        device_id=(partner, head), device_id_type=MESH,
    )

    core = head + 1 - 2 * lax.rem(head, 2)
    turn = lax.rem(seq // 2, 2)
    direct = across + turn * (1 - 2 * lax.rem(across, 2))
    mate = seq + 2 - 4 * turn

    def w_copy(step):
        if step == 2:
            source, target, place = w_all.at[direct], w_all.at[direct], (mate, head)
        else:
            peer = direct if step else core
            source = w_hbm.at[:, pl.ds(pl.multiple_of(peer * out_cols, LANES), out_cols)]
            target, place = w_all.at[head], (seq, peer)
        return send(source, target, w_send, w_recv.at[step], place)

    loads[0].wait()
    loads[1].wait()
    for i in range(n_bar):
        flag(i)
        prepare(give, i, theirs)
        prepare(own, i, mine)
        if i == 0:
            pl.semaphore_wait(barrier, count)
            bars_copy.start()
        give_copy(i).start()

        @pl.when(has_outer)
        def _(i=i):
            near_copy(i).start()

    for step in (1, 0):
        w_copy(step).start()

    def picks(table, c, turned):
        before = jnp.int32(0)
        chosen = [jnp.int32(0)] * CAP
        for b in range(n_bar):
            used = (table[b, c] >= 0).astype(jnp.int32)
            at = b + odd * (n_bar - 1 - 2 * b)
            if turned:
                at = n_bar - 1 - at
            for slot in range(CAP):
                chosen[slot] = chosen[slot] + jnp.where(before == slot, used * at, 0)
            before = before + used
        return chosen

    for slot, at in enumerate(picks(bars, column(columns - 1, columns), False)):
        pack_own[slot] = own[at]

    @pl.when(has_inner)
    def _():
        pick_copy(0).start()

    loads[2].wait()
    for i in range(n_bar):
        q_give[i] = (replaced(2, i, 0, theirs) * HD ** -0.5).astype(jnp.bfloat16)
    for i in range(n_bar):
        q_own[i] = (replaced(2, i, 0, mine) * HD ** -0.5).astype(jnp.bfloat16)

    @pl.when(jnp.logical_not(has_outer))
    def _():
        back[...] = jnp.zeros(back.shape, back.dtype)
        pick_near[...] = jnp.zeros(pick_near.shape, pick_near.dtype)

    @pl.when(jnp.logical_not(has_inner))
    def _():
        near[...] = jnp.zeros(near.shape, near.dtype)
        pick_far[...] = jnp.zeros(pick_far.shape, pick_far.dtype)

    for i in range(n_bar):
        give_copy(i).wait_recv()
        if i == 1:
            q_all.start()

        @pl.when(has_inner)
        def _(i=i):
            back_copy(i).start()

    bars_copy.wait_recv()
    for slot, at in enumerate(picks(twin_bars, column(0, columns), True)):
        pack_twin[slot] = twin[at]

    @pl.when(has_outer)
    def _():
        pick_copy(1).start()

    halves = [(lane // HD == h).astype(jnp.bfloat16) for h in range(per_tile)]

    def weigh(jobs):
        scores = []
        for query, blocks, _ in jobs:
            stacked = jnp.concatenate([query * half for half in halves], axis=0)
            row = []
            for block, usable in blocks:
                s = lax.dot_general(
                    stacked, block[:, :LANES], (((1,), (1,)), ((), ())), preferred_element_type=jnp.float32
                )
                if usable is not None:
                    s = s + jnp.where(usable, 0.0, NEG).astype(jnp.float32)
                row.append(s)
            scores.append(row)
        peaks, fades = [], []
        for row, (_, _, old) in zip(scores, jobs):
            peak = jnp.max(functools.reduce(jnp.maximum, row), axis=1, keepdims=True)
            if old is not None:
                peak = jnp.maximum(peak, top[old])
                fades.append(jnp.exp(top[old] - peak))
            else:
                fades.append(None)
            peaks.append(peak)
        totals, rounded = [], []
        for row, peak, fade, (_, _, old) in zip(scores, peaks, fades, jobs):
            raised = [jnp.exp(s - peak) for s in row]
            total = jnp.sum(functools.reduce(jnp.add, raised), axis=1, keepdims=True)
            if old is not None:
                total = total + tot[old] * fade
            totals.append(total)
            rounded.append(jnp.concatenate([r.astype(jnp.bfloat16) for r in raised], axis=1))
        sums = []
        for weight, fade, (_, blocks, old) in zip(rounded, fades, jobs):
            value = jnp.concatenate([block[:, LANES:] for block, _ in blocks], axis=0)
            weighted = jnp.dot(weight, value, preferred_element_type=jnp.float32)
            if old is not None:
                weighted = weighted + acc[old] * fade
            sums.append(weighted)
        return list(zip(peaks, totals, sums))

    def keep(slots, states):
        for slot, (peak, total, weighted) in zip(slots, states):
            top[slot] = jnp.broadcast_to(peak, top.shape[1:])
            tot[slot] = jnp.broadcast_to(total, tot.shape[1:])
            acc[slot] = weighted

    def finish(state):
        _, total, weighted = state
        done = weighted / total
        result = done[:bar_len]
        for h in range(1, per_tile):
            result = jnp.where(lane // HD == h, done[h * bar_len : (h + 1) * bar_len], result)
        return result.astype(jnp.bfloat16)

    def whole(table, b, c, ref, turned):
        wanted = table[b, c]
        at = lax.rem(jnp.maximum(wanted, 0), n_bar)
        at = at + odd * (n_bar - 1 - 2 * at)
        if turned:
            at = n_bar - 1 - at
        return ref[at], wanted >= 0

    def picked(table, b, c, ref):
        wanted = table[b, c]
        slot = jnp.int32(0)
        for o in range(n_bar):
            held = table[o, c]
            slot = slot + jnp.logical_and(held >= 0, held < wanted).astype(jnp.int32)
        return ref[jnp.minimum(slot, CAP - 1)], wanted >= 0

    def att_copy(order, i, kind):
        tile = odd + order * (1 - 2 * odd)
        slot = across if kind == 2 else head
        piece = att.at[slot, tile] if i is None else att.at[slot, tile, i]
        if order and kind != 1:
            recv = late_recv.at[i, kind // 2]
        else:
            recv = att_recv.at[order, i if kind == 1 else n_bar + kind // 2]
        return pltpu.make_async_remote_copy(
            src_ref=piece, dst_ref=piece, send_sem=att_send, recv_sem=recv,
            device_id=(seq, across if kind == 1 else core), device_id_type=MESH,
        )

    def y_copy(i):
        return send(att_twin.at[i], att.at[head, odd, i], y_send, y_recv.at[i], (partner, head))

    def corner_copy(i):
        return send(att_twin.at[i], att.at[head, odd, i], att_send, att_recv.at[1, i], (partner, across))

    def relay(order, i):
        att_copy(order, i, 1).wait_recv()
        att_copy(order, i, 2).start()

    @pl.when(has_outer)
    def _():
        pick_copy(0).wait_recv()

    @pl.when(has_inner)
    def _():
        near_all.wait_recv()

    last = n_bar - 1

    def band(mirror, i, beyond):
        blocks = [(mirror[n], None) for n in range(max(i - 1, 0), min(i + 2, n_bar))]
        if i == last:
            blocks.append((beyond[last], None))
        return blocks

    def own_first(i):
        b = slot_bar(i)
        blocks = band(own, i, twin)
        blocks.append(picked(bars, b, column(0, columns), pick_near))
        blocks.append(whole(bars, b, column(2, columns), twin, True))
        blocks.append(whole(bars, b, column(3, columns), near, False))
        return q_own[i], blocks, None

    def own_rest(i):
        blocks = [whole(bars, slot_bar(i), column(1, columns), back, True)]
        if i == 0:
            blocks.append((back[0], has_outer))
        return q_own[i], blocks, i

    def twin_bar(i):
        return last - i + odd * (2 * i - last)

    def twin_first(i):
        b = twin_bar(i)
        blocks = band(twin, i, own)
        if i == 0:
            blocks.append((near[0], has_inner))
        blocks.append(whole(twin_bars, b, column(1, columns), own, False))
        blocks.append(whole(twin_bars, b, column(2, columns), near, False))
        return q_twin[i], blocks, None

    def twin_rest(i):
        b = twin_bar(i)
        blocks = [whole(twin_bars, b, column(0, columns), back, True)]
        blocks.append(picked(twin_bars, b, column(3, columns), pick_far))
        return q_twin[i], blocks, n_bar + i

    slots = range(n_bar)
    keep(slots, weigh([own_first(i) for i in slots]))

    q_all.wait_recv()
    keep([n_bar + i for i in slots], weigh([twin_first(i) for i in slots]))

    @pl.when(has_outer)
    def _():
        back_all.wait_recv()

    def finish_own():
        for i, state in zip(slots, weigh([own_rest(i) for i in slots])):
            att[head, odd, i] = finish(state)
        for i in slots:
            att_copy(0, i, 1).start()
            att_copy(0, i, 0).start()

    pl.when(odd == 0)(finish_own)

    @pl.when(has_inner)
    def _():
        pick_copy(1).wait_recv()

    for i, state in zip(slots, weigh([twin_rest(i) for i in slots])):
        att_twin[i] = finish(state)
    for i in slots:
        corner_copy(i).start()
        y_copy(i).start()

    pl.when(odd == 1)(finish_own)
    w_copy(1).wait_recv()
    w_copy(2).start()

    def project(members, tile, span):
        lhs = jnp.concatenate([att[m, tile, span].reshape(-1, LANES) for m in members], axis=1)
        at = pl.ds(pl.multiple_of(tile * LANES, LANES), LANES)
        rhs = jnp.concatenate([w_all[m, at, :] for m in members], axis=0)
        return jnp.dot(lhs, rhs, preferred_element_type=jnp.float32)

    def forward(i):
        y_copy(i).wait_recv()
        att_copy(1, i, 0).start()
        relay(1, i)

    near_side, far_side = (head, across), (core, across + 1 - 2 * lax.rem(across, 2))
    every = slice(0, n_bar)
    for i in slots[: n_bar // 2]:
        relay(0, i)
    for i in slots[: n_bar // 2]:
        forward(i)
    for i in slots[n_bar // 2 :]:
        relay(0, i)
    own_w.wait()
    w_copy(0).wait_recv()
    w_copy(2).wait_recv()
    part[...] = project(near_side, odd, every)
    for i in slots[n_bar // 2 :]:
        forward(i)
    part[...] += project(near_side, other, every)
    att_copy(0, None, 0).wait_recv()
    att_copy(0, None, 2).wait_recv()
    part[...] += project(far_side, odd, every)
    for g in range(0, n_bar, GROUP):
        for i in slots[g : g + GROUP]:
            att_copy(1, i, 0).wait_recv()
            att_copy(1, i, 2).wait_recv()
        rest = project(far_side, other, slice(g, g + GROUP))
        for i in slots[g : g + GROUP]:
            row = (i - g) * bar_len
            whole_bar = part[i * bar_len : (i + 1) * bar_len] + rest[row : row + bar_len]
            out_ref[slot_bar(i)] = whole_bar.astype(jnp.bfloat16)

    bars_copy.wait_send()
    give_all.wait_send()
    q_all.wait_send()
    send(att_twin, att.at[head, odd], y_send, y_recv.at[0], (partner, head)).wait_send()
    sent = att.at[0 : n_head - 1]
    send(sent, sent, att_send, att_recv.at[0, 0], (seq, core)).wait_send()
    blocks = w_all.at[0:3]
    send(blocks, blocks, w_send, w_recv.at[0], (seq, core)).wait_send()

    @pl.when(has_outer)
    def _():
        near_all.wait_send()
        pick_copy(1).wait_send()

    @pl.when(has_inner)
    def _():
        back_all.wait_send()
        pick_copy(0).wait_send()


def solution(mesh):
    n_seq, n_head = mesh.shape["seq"], mesh.shape["head"]

    def on_device(queries, keys, values, masked, mask_qkv, key_bars, w_out):
        tokens, width = queries.shape
        bars, slots = key_bars.shape
        length = tokens // bars
        cols = w_out.shape[1] // n_head
        tiles = width // LANES
        shaped = [x.reshape(bars, length, width) for x in (queries, keys, values)]
        hbm = pl.BlockSpec(memory_space=pltpu.HBM)
        dma = pltpu.SemaphoreType.DMA
        bf16 = jnp.bfloat16
        pair = (bars, length, 2 * LANES)
        single = (bars, length, LANES)
        some = (CAP, length, 2 * LANES)
        out = pl.pallas_call(
            functools.partial(kernel, n_seq, n_head),
            out_shape=pltpu.VMEM((bars, length, cols), bf16),
            in_specs=[hbm] * 7,
            out_specs=pl.BlockSpec(memory_space=pltpu.VMEM),
            scratch_shapes=[
                pltpu.SMEM(key_bars.shape, jnp.int32),
                pltpu.SMEM(key_bars.shape, jnp.int32),
                pltpu.VMEM((bars, length), jnp.int32),
                pltpu.VMEM(mask_qkv.shape, bf16),
                pltpu.VMEM((3, bars, length, width), bf16),
            ]
            + [pltpu.VMEM(pair, bf16)] * 5
            + [pltpu.VMEM(some, bf16)] * 4
            + [pltpu.VMEM(single, bf16)] * 3
            + [
                pltpu.VMEM((n_head, width, cols), bf16),
                pltpu.VMEM((n_head, tiles, bars, length, LANES), bf16),
                pltpu.VMEM(single, bf16),
                pltpu.VMEM((tokens, cols), jnp.float32),
            ]
            + [pltpu.VMEM((2 * bars, LANES // HD * length, LANES), jnp.float32)] * 3
            + [
                dma((3,)),
                dma((3,)),
                dma,
                dma,
                dma,
                dma,
                dma((bars,)),
                dma,
                dma,
                dma,
                dma,
                dma,
                dma,
                dma((2,)),
                dma((2,)),
                dma,
                dma((3,)),
                dma,
                dma((bars,)),
                dma,
                dma((2, bars + 2)),
                dma((bars, 2)),
            ],
            compiler_params=pltpu.CompilerParams(
                collective_id=0, has_side_effects=True, vmem_limit_bytes=40 * 1024 * 1024
            ),
            name="bar_attention",
        )(*(pltpu.with_memory_space_constraint(x, pltpu.HBM) for x in (key_bars, masked.reshape(bars, length), mask_qkv, *shaped, w_out)))
        return out.reshape(tokens, cols)

    placed = (
        P("seq", "head"),
        P("seq", "head"),
        P("seq", "head"),
        P("seq"),
        P(None, "head"),
        P("seq", None),
        P("head", None),
    )
    return jax.shard_map(
        on_device, mesh=mesh, in_specs=placed, out_specs=P("seq", "head"), check_vma=False
    )
```
